256 devices in a mesh: pipe: 8 (over z), dp: 4 (over y), expert: 8 (over x, core).
Axes of the slice: x: 4, y: 4, z: 8, core: 2. Of those that a mesh axis runs over, the one named last changes fastest.
Arguments:
- tokens: bfloat16 [4096, 4096], P(('dp', 'expert'), 'pipe'), may hold values from -6 to 6
- routes: int32 [4096, 6], P(('dp', 'expert')), may hold values from 0 to 31, all different within a row; in each aligned block of 128 rows (0 to 127, 128 to 255, ...) at most 32 rows name the same one
- gates: float32 [4096, 6], P(('dp', 'expert')), may hold values from 0.1 to 0.5
- w_gate: bfloat16 [32, 4096, 1024], P(('dp', 'expert'), 'pipe'), may hold values from -0.09375 to 0.09375
- w_up: bfloat16 [32, 4096, 1024], P(('dp', 'expert'), 'pipe'), may hold values from -0.09375 to 0.09375
- w_down: bfloat16 [32, 1024, 4096], P(('dp', 'expert'), None, 'pipe'), may hold values from -0.1875 to 0.1875
- grad_out: bfloat16 [4096, 4096], P(('dp', 'expert'), 'pipe'), may hold values from -6 to 6
Outputs:
- mixed: bfloat16 [4096, 4096], P(('dp', 'expert'), 'pipe')
- grad_tokens: bfloat16 [4096, 4096], P(('dp', 'expert'), 'pipe')
- grad_gate: bfloat16 [32, 4096, 1024], P(('dp', 'expert'), 'pipe')
- grad_up: bfloat16 [32, 4096, 1024], P(('dp', 'expert'), 'pipe')
- grad_down: bfloat16 [32, 1024, 4096], P(('dp', 'expert'), None, 'pipe')
The draws below stay inside these ranges and needn't reach their ends.
Inputs may be any that keep to these rules, and one draw needn't show every extreme that they name: `routes`: each row names 6 different experts; in each aligned block of 128 rows no expert is named by more than 32 rows, a bound that some block reaches.
All inputs are finite; a program needn't handle non-finite values.
Results may differ from the reference program's by a relative error of at most 0.0065.
Values may be sent and summed in bfloat16 or wider, within the bound.
A program may use at most 128 MiB of HBM per device.

```python
import math
import jax
import jax.numpy as jnp
import numpy as np
from jax import lax

D = 4096
FF = 1024
EXPERTS = 32
TOP = 6
TOK_DEV = 128
CAP = 32
TOKENS = 4096


def levels(own_key, dims, pieces, smallest, top_value):
    def one(dim, parts):
        steps = jax.random.uniform(jax.random.fold_in(jax.random.fold_in(own_key, 6), dim), (parts,), jnp.float32, smallest / len(pieces), top_value / len(pieces))
        return jnp.repeat(jnp.exp(steps), dims[dim] // parts).reshape((-1,) + (1,) * (len(dims) - dim - 1))

    factor_of = one(*pieces[0])
    for cut in pieces[1:]:
        factor_of = factor_of * one(*cut)
    return factor_of


def deal_out(key, own, number, rows, number_of, top, reach, lean):
    ranking = jax.random.permutation(key, number_of)
    packed, common = load_shares(number_of, rows * top, reach, lean, True), load_shares(number_of, rows * top, reach, lean, False)
    places = jnp.arange(number_of)

    def named(tallies, rotation):
        used = int((tallies > 0).sum())
        fixed = max(1, used // 4)
        moved = fixed + (places - fixed + rotation * (used - fixed)) % max(1, number_of - fixed)
        return jnp.zeros((number_of,), jnp.int32).at[ranking[jnp.where(places < fixed, places, moved)]].set(jnp.asarray(tallies, jnp.int32))

    tallies = jnp.where(number % 4 == 0, named(packed, number // 4), named(common, number - number // 4 - 1))
    mixed = jax.random.permutation(jax.random.fold_in(own, 3), number_of)
    donor, taker = mixed[0:number_of // 2 * 2:2], mixed[1:number_of // 2 * 2:2]
    margin = jnp.minimum(tallies[donor] - 1, reach - tallies[taker]) // 2
    margin = jnp.where((donor == ranking[0]) | (taker == ranking[0]) | (tallies[taker] == 0), 0, jnp.maximum(margin, 0))
    moved = jax.random.randint(jax.random.fold_in(own, 4), (number_of // 2,), 0, 1 << 20) % (margin + 1)
    tallies = tallies.at[donor].add(-moved).at[taker].add(moved)
    members = jnp.searchsorted(jnp.cumsum(tallies), jnp.arange(rows * top), side="right").astype(jnp.int32)
    table = members.reshape(top, rows).T
    table = table[jax.random.permutation(jax.random.fold_in(own, 1), rows)]
    rotation = jax.random.randint(jax.random.fold_in(own, 2), (rows, 1), 0, top)
    return jnp.take_along_axis(table, (jnp.arange(top)[None, :] + rotation) % top, axis=1)


def load_shares(amount, total, bound, skew, full):
    portions = [(1 << 20) // math.isqrt(grade ** skew) + 1 for grade in range(1, amount + 1)]
    largest = bound if full else min(bound, max(-(-total // amount), total * portions[0] // sum(portions)))
    least = 1 if total - largest >= amount - 1 else 0
    counts, surplus = [largest] + [least] * (amount - 1), total - largest - least * (amount - 1)
    while surplus > 0:
        movable = [i for i in range(1, amount) if counts[i] < largest] or [i for i in range(1, amount) if counts[i] < bound]
        mass, left = sum([portions[i] for i in movable]), surplus
        for i in movable:
            extra = min(bound - counts[i], max(1, left * portions[i] // mass), surplus)
            counts[i] = counts[i] + extra
            surplus = surplus - extra
    return np.array(counts)


def normal_values(own_key, dims, deviation, reach, pieces=(), held_as=jnp.bfloat16):
    factor_of = levels(own_key, dims, pieces, -0.22, 0.18) if pieces else 1.0
    values = jax.random.normal(own_key, dims, jnp.float32) * deviation * factor_of
    return jnp.minimum(jnp.maximum(values, -reach), reach).astype(held_as)


def setup_inputs(seed: int = 0) -> dict:
    keys = jax.random.split(jax.random.key(seed), 8)
    tokens = normal_values(keys[0], (TOKENS, D), 1.0, 6.0, ((0, 32), (1, 8)))
    routes_keys = jax.random.split(jax.random.fold_in(keys[1], 1), TOKENS // TOK_DEV)
    routes_turns = jax.random.permutation(jax.random.fold_in(keys[1], 3), TOKENS // TOK_DEV)
    routes = jax.vmap(lambda own, number: deal_out(jax.random.fold_in(keys[1], 2), own, number, TOK_DEV, EXPERTS, TOP, CAP, 2))(routes_keys, routes_turns).reshape((TOKENS, TOP))
    gates = jnp.clip(0.1 + 0.4 * jax.random.uniform(keys[2], (TOKENS, TOP), jnp.float32) ** levels(keys[2], (TOKENS, TOP), ((0, 32),), -0.2, 0.2), 0.1, 0.5)
    w_gate = normal_values(keys[3], (EXPERTS, D, FF), D ** -0.5, 0.09375, ((0, 32), (1, 8)))
    w_up = normal_values(keys[4], (EXPERTS, D, FF), D ** -0.5, 0.09375, ((0, 32), (1, 8)))
    w_down = normal_values(keys[5], (EXPERTS, FF, D), FF ** -0.5, 0.1875, ((0, 32), (2, 8)))
    grad_out = normal_values(keys[6], (TOKENS, D), 1.0, 6.0, ((0, 32), (1, 8)))
    return {"tokens": tokens, "routes": routes, "gates": gates, "w_gate": w_gate, "w_up": w_up, "w_down": w_down, "grad_out": grad_out}


def reference(tokens, routes, gates, w_gate, w_up, w_down, grad_out):
    num_blocks = TOKENS // TOK_DEV
    per_block = TOK_DEV * TOP
    chosen = routes.reshape(num_blocks, per_block)
    gate_flat = gates.reshape(num_blocks, per_block)
    expert_ids = jnp.arange(EXPERTS, dtype=jnp.int32)
    onehot = (chosen[:, :, None] == expert_ids[None, None, :]).astype(jnp.int32)
    earlier = jnp.cumsum(onehot, axis=1) - onehot
    position = jnp.sum(earlier * onehot, axis=2)
    token_of = jnp.arange(per_block, dtype=jnp.int32) // TOP
    block_start = (jnp.arange(num_blocks, dtype=jnp.int32) * TOK_DEV)[:, None]
    slot_ids = jnp.arange(CAP, dtype=jnp.int32)

    def one_expert(state, inputs):
        y_total, dx_total = state
        expert_id, wg_e, wu_e, wd_e = inputs
        hits = (chosen == expert_id)[:, None, :] & (position[:, None, :] == slot_ids[None, :, None])
        row_token = (jnp.sum(jnp.where(hits, token_of[None, None, :], 0), axis=2) + block_start)
        row_token = row_token.reshape(num_blocks * CAP).astype(jnp.int32)
        row_gate = jnp.sum(jnp.where(hits, gate_flat[:, None, :], 0.0), axis=2).reshape(num_blocks * CAP)
        x_rows = tokens[row_token]
        gate_val = jnp.dot(x_rows, wg_e, preferred_element_type=jnp.float32)
        up_val = jnp.dot(x_rows, wu_e, preferred_element_type=jnp.float32)
        hidden = (jax.nn.silu(gate_val) * up_val).astype(jnp.bfloat16)
        expert_out = jnp.dot(hidden, wd_e, preferred_element_type=jnp.float32).astype(jnp.bfloat16)
        y_total = y_total.at[row_token].add(row_gate[:, None] * expert_out.astype(jnp.float32))
        scaled = (row_gate[:, None] * grad_out[row_token].astype(jnp.float32)).astype(jnp.bfloat16)
        d_hidden = jnp.dot(scaled, wd_e.T, preferred_element_type=jnp.float32)
        sig_gate = jax.nn.sigmoid(gate_val)
        d_gate = (d_hidden * up_val * sig_gate * (1.0 + gate_val * (1.0 - sig_gate))).astype(jnp.bfloat16)
        d_up = (d_hidden * gate_val * sig_gate).astype(jnp.bfloat16)
        d_rows = (jnp.dot(d_gate, wg_e.T, preferred_element_type=jnp.float32)
                  + jnp.dot(d_up, wu_e.T, preferred_element_type=jnp.float32)).astype(jnp.bfloat16)
        dx_total = dx_total.at[row_token].add(d_rows.astype(jnp.float32))
        grads = (jnp.dot(x_rows.T, d_gate, preferred_element_type=jnp.float32).astype(jnp.bfloat16),
                 jnp.dot(x_rows.T, d_up, preferred_element_type=jnp.float32).astype(jnp.bfloat16),
                 jnp.dot(hidden.T, scaled, preferred_element_type=jnp.float32).astype(jnp.bfloat16))
        return (y_total, dx_total), grads

    start_state = (jnp.zeros((TOKENS, D), jnp.float32), jnp.zeros((TOKENS, D), jnp.float32))
    final_state, grads = lax.scan(one_expert, start_state, (expert_ids, w_gate, w_up, w_down))
    mixed = final_state[0].astype(jnp.bfloat16)
    grad_tokens = final_state[1].astype(jnp.bfloat16)
    return (mixed, grad_tokens, grads[0], grads[1], grads[2])
```

```python
import jax
import jax.numpy as jnp
from jax import lax
from jax.sharding import PartitionSpec as P

CAP = 32


def slot_layout(routes, num_experts):
    tok_count, top_count = routes.shape
    chosen = routes.reshape(tok_count * top_count)
    expert_ids = jnp.arange(num_experts, dtype=jnp.int32)
    onehot = (chosen[:, None] == expert_ids[None, :]).astype(jnp.int32)
    earlier = jnp.cumsum(onehot, axis=0) - onehot
    position = jnp.sum(earlier * onehot, axis=1)
    target = chosen * CAP + position
    slot_ids = jnp.arange(num_experts * CAP, dtype=jnp.int32)
    placed = slot_ids[:, None] == target[None, :]
    return placed.reshape(num_experts * CAP, tok_count, top_count)


def arc_sum(part, sign):
    size = lax.axis_size("pipe")
    me = lax.axis_index("pipe")
    pieces = part.reshape((size, part.shape[0] // size) + part.shape[1:])

    def own(offset):
        return lax.dynamic_index_in_dim(pieces, (me + offset) % size, 0, keepdims=False)

    def arc(direction, hops):
        perm = [(i, (i + direction) % size) for i in range(size)]
        moving = own(direction * hops).astype(jnp.bfloat16)
        for left in range(hops - 1, -1, -1):
            moving = lax.ppermute(moving, "pipe", perm)
            if left:
                moving = (moving.astype(jnp.float32) + own(direction * left)).astype(jnp.bfloat16)
        return moving.astype(jnp.float32)

    far = size // 2
    return own(0) + arc(sign, far) + arc(-sign, size - 1 - far)


def local(tokens, routes, gates, w_gate, w_up, w_down, grad_out):
    groups = lax.axis_size(("dp", "expert"))
    local_experts = w_gate.shape[0]
    num_experts = local_experts * groups
    slice_width = tokens.shape[1]
    placed = slot_layout(routes, num_experts)
    dispatch = jnp.sum(placed.astype(jnp.int32), axis=2).astype(jnp.bfloat16)
    mixing = jnp.sum(jnp.where(placed, gates[None, :, :], 0.0), axis=2)
    outbound = jnp.dot(dispatch, tokens, preferred_element_type=jnp.float32).astype(jnp.bfloat16)
    outbound = outbound.reshape(num_experts, CAP, slice_width)
    scaled_out = jnp.dot(
        mixing, grad_out.astype(jnp.float32), precision=lax.Precision.HIGHEST
    ).astype(jnp.bfloat16)
    scaled_out = scaled_out.reshape(num_experts, CAP, slice_width)
    arrived, arrived_grad = (
        lax.all_to_all(outbound, ("dp", "expert"), split_axis=0, concat_axis=0, tiled=True),
        lax.all_to_all(scaled_out, ("dp", "expert"), split_axis=0, concat_axis=0, tiled=True),
    )
    expert_rows = arrived.reshape(groups, local_experts, CAP, slice_width)
    scaled = arrived_grad.reshape(groups, local_experts, CAP, slice_width)
    gate_part = jnp.einsum(
        "sjcd,jdf->sjcf", expert_rows, w_gate, preferred_element_type=jnp.float32
    )
    up_part = jnp.einsum("sjcd,jdf->sjcf", expert_rows, w_up, preferred_element_type=jnp.float32)
    gate_share, up_share = (
        arc_sum(gate_part, 1),
        arc_sum(up_part, -1),
    )
    hidden_share = (jax.nn.silu(gate_share) * up_share).astype(jnp.bfloat16)
    hidden = lax.all_gather(hidden_share, "pipe", axis=0, tiled=True)
    expert_out = jnp.einsum(
        "sjcf,jfd->sjcd", hidden, w_down, preferred_element_type=jnp.float32
    ).astype(jnp.bfloat16)
    returned = lax.all_to_all(
        expert_out.reshape(num_experts, CAP, slice_width),
        ("dp", "expert"),
        split_axis=0,
        concat_axis=0,
        tiled=True,
    )
    returned_rows = returned.reshape(num_experts * CAP, slice_width).astype(jnp.float32)
    mixed = jnp.dot(mixing.T, returned_rows, precision=lax.Precision.HIGHEST).astype(jnp.bfloat16)
    d_hidden_part = jnp.einsum("sjcd,jfd->sjcf", scaled, w_down, preferred_element_type=jnp.float32)
    d_hidden = arc_sum(d_hidden_part, 1)
    sig_gate = jax.nn.sigmoid(gate_share)
    d_gate_share = (d_hidden * up_share * sig_gate * (1.0 + gate_share * (1.0 - sig_gate))).astype(
        jnp.bfloat16
    )
    d_up_share = (d_hidden * gate_share * sig_gate).astype(jnp.bfloat16)
    d_gate, d_up = (
        lax.all_gather(d_gate_share, "pipe", axis=0, tiled=True),
        lax.all_gather(d_up_share, "pipe", axis=0, tiled=True),
    )
    d_rows = (
        jnp.einsum("sjcf,jdf->sjcd", d_gate, w_gate, preferred_element_type=jnp.float32)
        + jnp.einsum("sjcf,jdf->sjcd", d_up, w_up, preferred_element_type=jnp.float32)
    ).astype(jnp.bfloat16)
    back_rows = lax.all_to_all(
        d_rows.reshape(num_experts, CAP, slice_width),
        ("dp", "expert"),
        split_axis=0,
        concat_axis=0,
        tiled=True,
    )
    grad_tokens = jnp.dot(
        dispatch.T,
        back_rows.reshape(num_experts * CAP, slice_width),
        preferred_element_type=jnp.float32,
    ).astype(jnp.bfloat16)
    grad_gate = jnp.einsum(
        "sjcd,sjcf->jdf", expert_rows, d_gate, preferred_element_type=jnp.float32
    ).astype(jnp.bfloat16)
    grad_up = jnp.einsum(
        "sjcd,sjcf->jdf", expert_rows, d_up, preferred_element_type=jnp.float32
    ).astype(jnp.bfloat16)
    grad_down = jnp.einsum(
        "sjcf,sjcd->jfd", hidden, scaled, preferred_element_type=jnp.float32
    ).astype(jnp.bfloat16)
    return (mixed, grad_tokens, grad_gate, grad_up, grad_down)


def solution(mesh):
    placed = (
        P(("dp", "expert"), "pipe"),
        P(("dp", "expert"), None),
        P(("dp", "expert"), None),
        P(("dp", "expert"), "pipe", None),
        P(("dp", "expert"), "pipe", None),
        P(("dp", "expert"), None, "pipe"),
        P(("dp", "expert"), "pipe"),
    )
    return jax.shard_map(
        local,
        mesh=mesh,
        in_specs=placed,
        out_specs=(
            P(("dp", "expert"), "pipe"),
            P(("dp", "expert"), "pipe"),
            P(("dp", "expert"), "pipe", None),
            P(("dp", "expert"), "pipe", None),
            P(("dp", "expert"), None, "pipe"),
        ),
        check_vma=False,
    )
```
